32 devices in a mesh: tm: 2 (over y), height: 16 (over z, x, core).
Axes of the slice: x: 2, y: 2, z: 4, core: 2. Of those that a mesh axis runs over, the one named last changes fastest.
Arguments:
- activations: bfloat16 [4, 64, 256, 128], P('tm', 'height'), may hold values from -60 to 60
- norm_gain: float32 [128], replicated, may hold values from 0.1 to 1.9
- norm_bias: float32 [128], replicated, may hold values from -3 to 3
- conv_weight: bfloat16 [3456, 256], replicated, may hold values from -0.109375 to 0.109375
- cotangent: bfloat16 [2, 64, 256, 256], P('tm', 'height'), may hold values from -6 to 6
Outputs:
- pooled: bfloat16 [2, 64, 256, 256], P('tm', None, 'height')
- weight_grad: bfloat16 [256, 3456], P('height')
The draws below stay inside these ranges and needn't reach their ends.
All inputs are finite; a program needn't handle non-finite values.
Results may differ from the reference program's by a relative error of at most 0.0056.
Values may be sent and summed in bfloat16 or wider, within the bound.
A program may use at most 128 MiB of HBM per device.

```python
import math
import jax
import jax.numpy as jnp
from jax import lax

CIN = 128
COUT = 256
GROUPS = 32
KT = 3
W_COLS = 256
FRAMES = 4
ROWS = 64
FO = 2


def draw_activations(key, part):
    key_noise, key_rough, key_offset, key_factor, key_drift = jax.random.split(key, 5)
    frame_pos = jnp.arange(FRAMES, dtype=jnp.float32) / FRAMES
    row_pos = jnp.arange(ROWS, dtype=jnp.float32) / ROWS
    col_pos = jnp.arange(W_COLS, dtype=jnp.float32) / W_COLS
    level = (frame_pos[:, None, None] + row_pos[None, :, None] + col_pos[None, None, :]) / 3.0
    rough = jax.random.uniform(key_rough, (FRAMES, ROWS, W_COLS), jnp.float32, -0.35, 0.35)
    scale = jnp.exp(2.302585 * level + rough)
    group_factor = jax.random.uniform(key_factor, (GROUPS,), jnp.float32, 0.5, 1.0)
    chan_factor = jnp.repeat(group_factor, CIN // GROUPS)
    amplitude = jax.random.uniform(key_drift, (CIN,), jnp.float32, 0.5, 2.0)
    drift = (frame_pos[:, None, None, None] + row_pos[None, :, None, None]) * 0.5 * amplitude
    noise = jnp.clip(jax.random.normal(key_noise, (FRAMES, ROWS, W_COLS, CIN), jnp.float32), -3.5, 3.5)
    offset = jax.random.uniform(key_offset, (CIN,), jnp.float32, -1.0, 1.0)
    values = noise * scale[:, :, :, None] * chan_factor + offset + drift
    return values.astype(jnp.bfloat16)


def shard_levels(own_key, shape, cuts, least, top_value):
    factor_of = 1.0
    for position, blocks in cuts:
        steps = jax.random.uniform(jax.random.fold_in(jax.random.fold_in(own_key, 6), position), (blocks,), jnp.float32, least / len(cuts), top_value / len(cuts))
        factor_of = factor_of * jnp.repeat(jnp.exp(steps), shape[position] // blocks).reshape((-1,) + (1,) * (len(shape) - 1 - position))
    return factor_of


def centred(key, dims, deviation, bound, cuts=(), kind=jnp.bfloat16):
    array = deviation * jax.random.normal(key, dims, jnp.float32)
    if cuts:
        array = array * shard_levels(key, dims, cuts, -0.22, 0.18)
    return jnp.clip(array, -bound, bound).astype(kind)


def setup_inputs(seed: int = 0) -> dict:
    key_list = jax.random.split(jax.random.key(seed), 6)
    return {
        "activations": draw_activations(jax.random.fold_in(key_list[5], 71), 0),
        "norm_gain": jnp.clip(1.0 + 0.18 * jax.random.normal(key_list[1], (CIN,), jnp.float32), 0.1, 1.9),
        "norm_bias": centred(key_list[2], (CIN,), 0.5, 3.0, (), jnp.float32),
        "conv_weight": centred(key_list[3], (KT * KT * KT * CIN, COUT), (KT * KT * KT * CIN) ** -0.5, 0.109375),
        "cotangent": centred(key_list[4], (FO, ROWS, W_COLS, COUT), 1.0, 6.0, ((0, 2), (1, 16))),
    }


def reference(activations, norm_gain, norm_bias, conv_weight, cotangent):
    per_group = CIN // GROUPS
    grouped = activations.astype(jnp.float32).reshape(-1, GROUPS, per_group)
    group_mean = lax.optimization_barrier(jnp.mean(grouped, axis=(0, 2)))
    centered = grouped - group_mean[None, :, None]
    group_var = lax.optimization_barrier(jnp.mean(centered * centered, axis=(0, 2)))
    mean_chan = jnp.repeat(group_mean, per_group)
    inv_chan = jnp.repeat(lax.rsqrt(group_var + 1e-06), per_group)
    normed = jax.nn.silu((activations.astype(jnp.float32) - mean_chan) * inv_chan * norm_gain + norm_bias).astype(jnp.bfloat16)
    stacked = jnp.concatenate([normed[:1], normed[:1], normed], axis=0)
    padded = jnp.pad(stacked, ((0, 0), (1, 1), (1, 1), (0, 0)))
    upsampled = jnp.repeat(cotangent * jnp.asarray(0.5, jnp.bfloat16), 2, axis=0)

    def frame_step(total, index):
        window = lax.dynamic_slice_in_dim(padded, index, KT, 0)
        pieces = []
        for tap_t in range(KT):
            for tap_r in range(KT):
                for tap_c in range(KT):
                    pieces.append(window[tap_t, tap_r:tap_r + ROWS, tap_c:tap_c + W_COLS])
        patches = jnp.concatenate(pieces, axis=2).reshape(ROWS * W_COLS, KT * KT * KT * CIN)
        frame_out = jnp.dot(patches, conv_weight, preferred_element_type=jnp.float32).astype(jnp.bfloat16)
        upstream = lax.dynamic_index_in_dim(upsampled, index, 0, keepdims=False).reshape(ROWS * W_COLS, COUT)
        total = total + jnp.dot(patches.T, upstream, preferred_element_type=jnp.float32)
        return (total, frame_out.reshape(ROWS, W_COLS, COUT))
    total, conv_out = lax.scan(frame_step, jnp.zeros((KT * KT * KT * CIN, COUT), jnp.float32), jnp.arange(FRAMES, dtype=jnp.int32))
    pairs = conv_out.reshape(FO, 2, ROWS, W_COLS, COUT).astype(jnp.float32)
    pooled = ((pairs[:, 0] + pairs[:, 1]) * 0.5).astype(jnp.bfloat16).transpose(0, 1, 3, 2)
    weight_grad = (total.T * (1.0 / math.sqrt(FRAMES * ROWS * W_COLS))).astype(jnp.bfloat16)
    return (pooled, weight_grad)
```

```python
import functools
import math

import jax
import jax.numpy as jnp
from jax import lax
from jax.experimental import pallas as pl
from jax.experimental.pallas import tpu as pltpu
from jax.sharding import PartitionSpec as P

GROUPS = 32
KT = 3
MESH = pl.DeviceIdType.MESH
VMEM = pl.BlockSpec(memory_space=pltpu.VMEM)
BF16 = jnp.bfloat16
F32 = jnp.float32


def group_total(row, per_group):
    lane = lax.broadcasted_iota(jnp.int32, row.shape, 1)
    count = row.shape[1]
    span = 1
    while span < per_group:
        low = (lane % (2 * span)) < span
        row = row + jnp.where(low, pltpu.roll(row, count - span, 1), pltpu.roll(row, span, 1))
        span *= 2
    return row


def gather_kernel(n_time, n_rows, act, full, scale, mine, stats, halo_send, halo_recv, stat_send, stat_recv):
    time, height = lax.axis_index("tm"), lax.axis_index("height")
    frames, rows, width, channels = act.shape
    n_dev = n_time * n_rows
    me = time * n_rows + height

    barrier = pltpu.get_barrier_semaphore()

    def greet(step, carry):
        other = (me + step) % n_dev
        pl.semaphore_signal(barrier, inc=1, device_id=(other // n_rows, other % n_rows), device_id_type=MESH)
        return carry

    lax.fori_loop(1, n_dev, greet, 0)
    pl.semaphore_wait(barrier, n_dev - 1)

    top, bottom = pl.ds(0, 1), pl.ds(rows - 1, 1)
    has_up, has_down = height > 0, height < n_rows - 1
    has_next, has_prev = time < n_time - 1, time > 0
    up, down = height - 1, height + 1
    own, old = pl.ds(frames, frames), pl.ds(0, frames)
    everything = pl.ds(0, rows)
    moves = [
        (1, 0, everything, old, pl.ds(1, rows), has_next, has_prev),
        (1, -1, top, old, pl.ds(rows + 1, 1), has_next & has_up, has_prev & has_down),
        (1, 1, bottom, old, pl.ds(0, 1), has_next & has_down, has_prev & has_up),
        (0, -1, top, own, pl.ds(rows + 1, 1), has_up, has_down),
        (0, 1, bottom, own, pl.ds(0, 1), has_down, has_up),
    ]

    def halo(index):
        frame_step, row_step, source, to_frames, to_rows, sends, receives = moves[index]
        copy = pltpu.make_async_remote_copy(
            src_ref=act.at[:, source],
            dst_ref=full.at[to_frames, to_rows],
            send_sem=halo_send.at[index],
            recv_sem=halo_recv.at[index],
            device_id=(time + frame_step, height + row_step),
            device_id_type=MESH,
        )
        return copy, sends, receives

    for index in range(len(moves)):
        copy, sends, _ = halo(index)
        pl.when(sends)(copy.start)

    local = frames * rows * width
    chan_sum = jnp.zeros((1, channels), F32)
    for f in range(frames):
        for r in range(rows):
            chan_sum = chan_sum + jnp.sum(act[f, r].astype(F32), axis=0, keepdims=True)
    chan_mean = chan_sum * (1.0 / local)
    chan_dev = jnp.zeros((1, channels), F32)
    for f in range(frames):
        for r in range(rows):
            away = act[f, r].astype(F32) - chan_mean
            chan_dev = chan_dev + jnp.sum(away * away, axis=0, keepdims=True)
    packed = jnp.concatenate([chan_mean, chan_dev, jnp.zeros((6, channels), F32)], axis=0)
    mine[...] = packed
    stats[me] = packed

    def stat(step, slot, other):
        return pltpu.make_async_remote_copy(
            src_ref=mine,
            dst_ref=stats.at[slot],
            send_sem=stat_send.at[step],
            recv_sem=stat_recv.at[step],
            device_id=(other // n_rows, other % n_rows),
            device_id_type=MESH,
        )

    def send(step, carry):
        stat(step, me, (me + step) % n_dev).start()
        return carry

    lax.fori_loop(1, n_dev, send, 0)

    full[pl.ds(frames, frames), pl.ds(1, rows)] = act[...]
    zero_rows = jnp.zeros((2 * frames, 1, width, channels), BF16)

    @pl.when(jnp.logical_not(has_up))
    def _():
        full[:, pl.ds(0, 1)] = zero_rows

    @pl.when(jnp.logical_not(has_down))
    def _():
        full[:, pl.ds(rows + 1, 1)] = zero_rows

    def receive(step, carry):
        from_dev = (me + n_dev - step) % n_dev
        stat(step, from_dev, from_dev).wait_recv()
        return carry

    lax.fori_loop(1, n_dev, receive, 0)
    per_group = channels // GROUPS
    means, devs = stats[:, 0], stats[:, 1]
    mean = group_total(jnp.sum(means, axis=0, keepdims=True), per_group) * (1.0 / (n_dev * per_group))
    away = means - mean
    spread = jnp.sum(devs + local * (away * away), axis=0, keepdims=True)
    var = group_total(spread, per_group) * (1.0 / (local * n_dev * per_group))
    scale[...] = jnp.concatenate([mean, lax.rsqrt(var + 1e-06), jnp.zeros((6, channels), F32)], axis=0)

    for index in range(len(moves)):
        copy, sends, receives = halo(index)
        pl.when(receives)(copy.wait_recv)
        pl.when(sends)(copy.wait_send)

    @pl.when(jnp.logical_not(has_prev))
    def _():
        first = full[frames]
        for f in range(frames):
            full[f] = first

    def sent(step, carry):
        stat(step, me, (me + step) % n_dev).wait_send()
        return carry

    lax.fori_loop(1, n_dev, sent, 0)


def compute_kernel(dims, full, scale, gain, bias, weight, cot, pooled, grad, taps, cot_t):
    n_time, n_rows, outer, inner = dims
    height = lax.axis_index("height")
    n_pad, width, channels = full.shape[1:]
    rows = n_pad - 2
    n_out = weight.shape[1]
    own_rows = n_out // n_rows
    mean, factor, bias_row = scale[0:1], scale[1:2] * gain[...], bias[...]
    column = lax.broadcasted_iota(jnp.int32, (width, channels), 0)

    def prepare(r, carry):
        inside = jnp.logical_and(r + height > 0, r + height * rows < n_rows * rows + 1)
        keep = inside.astype(F32)

        def normed(f):
            v = (full[f, r].astype(F32) - mean) * factor + bias_row
            v = v / (1.0 + jnp.exp(-v))
            return v.astype(BF16).astype(F32) * keep

        frames = [normed(f) for f in range(4)]
        for t in range(KT):
            pair = frames[t] + frames[t + 1]
            left = jnp.where(column == 0, 0.0, pltpu.roll(pair, 1, 0))
            right = jnp.where(column == width - 1, 0.0, pltpu.roll(pair, width - 1, 0))
            base = pl.ds(pl.multiple_of(r * width, width), width)
            taps[t, base, 0:channels] = left.astype(BF16)
            taps[t, base, channels : 2 * channels] = pair.astype(BF16)
            taps[t, base, 2 * channels :] = right.astype(BF16)
        return carry

    lax.fori_loop(0, n_pad, prepare, 0)

    def conv(y, carry):
        patch = jnp.concatenate(
            [taps[t, pl.ds(pl.multiple_of((y + r) * width, width), width)] for t in range(KT) for r in range(KT)], axis=1
        )
        out = jnp.dot(patch, weight[...], preferred_element_type=F32) * 0.5
        pooled[:, y] = out.T.astype(BF16).reshape(n_rows, own_rows, width)
        cot_t[:, pl.ds(pl.multiple_of(y * width, width), width)] = cot[y].astype(F32).T.astype(BF16)
        return carry

    lax.fori_loop(0, rows, conv, 0)
    span = grad.shape[-1]
    upstream = cot_t[...]
    pixels = rows * width
    band = KT * KT * channels
    for t in range(KT):
        rhs = jnp.concatenate([taps[t, pl.ds(r * width, pixels)] for r in range(KT)], axis=1)
        total = jnp.dot(upstream, rhs, preferred_element_type=F32).astype(BF16)
        for piece in range(n_time):
            first, last = max(t * band, piece * span), min((t + 1) * band, (piece + 1) * span)
            if first < last:
                part = total[:, first - t * band : last - t * band]
                for block in range(n_rows):
                    q, core = block // 2, block % 2
                    grad[core, piece, q % inner, q // inner, :, first - piece * span : last - piece * span] = part[
                        block * own_rows : (block + 1) * own_rows
                    ]
    extra = n_time * span - KT * band
    if extra:
        for piece in range(n_time):
            first = max(KT * band, piece * span) - piece * span
            if first < span:
                grad[:, piece, :, :, :, first:] = jnp.zeros((2, inner, outer, own_rows, span - first), BF16)


def scatter_kernel(
    dims, factor, pooled, grad, out, wgrad, got1, sum1, got2, sum2, got3, part, sems_a, semr_a, sems, semr, final
):
    n_time, n_rows, outer, inner = dims
    time, height = lax.axis_index("tm"), lax.axis_index("height")
    core, q = height % 2, height // 2
    b, a = q % inner, q // inner
    rows = pooled.shape[1]

    def index_of(a_, b_, c_):
        return (a_ * inner + b_) * 2 + c_

    def remote(src, dst, index, to):
        return pltpu.make_async_remote_copy(
            src_ref=src, dst_ref=dst, send_sem=sems.at[index], recv_sem=semr.at[index], device_id=to, device_id_type=MESH
        )

    barrier = pltpu.get_barrier_semaphore()
    for step in range(1, n_rows):
        pl.semaphore_signal(barrier, inc=1, device_id=(time, (height + step) % n_rows), device_id_type=MESH)
    for t in range(1, n_time):
        for b_ in range(inner):
            pl.semaphore_signal(
                barrier, inc=1, device_id=((time + t) % n_time, index_of(a, b_, core)), device_id_type=MESH
            )
    pl.semaphore_wait(barrier, n_rows - 1 + (n_time - 1) * inner)

    pair = remote(grad.at[1 - core], got1, 0, (time, index_of(a, b, 1 - core)))
    pair.start()

    def block(step, slot, other):
        return pltpu.make_async_remote_copy(
            src_ref=pooled.at[other],
            dst_ref=out.at[pl.ds(slot * rows, rows)],
            send_sem=sems_a.at[step],
            recv_sem=semr_a.at[step],
            device_id=(time, other),
            device_id_type=MESH,
        )

    for step in range(1, n_rows):
        block(step, height, (height + step) % n_rows).start()
    out[pl.ds(height * rows, rows)] = pooled[height]

    pair.wait()
    for t in range(n_time):
        for b_ in range(inner):
            for a_ in range(outer):
                sum1[t, b_, a_] = (grad[core, t, b_, a_].astype(F32) + got1[t, b_, a_].astype(F32)).astype(BF16)

    def second(dt, db, backward):
        sign = -1 if backward else 1
        t_, b_ = (time + n_time + sign * dt) % n_time, (b + inner + sign * db) % inner
        slot = dt * inner + db - 1
        return remote(sum1.at[t_, b_], got2.at[slot], 1 + slot, (t_, index_of(a, b_, core)))

    group = [(dt, db) for dt in range(n_time) for db in range(inner) if dt or db]
    seconds = [second(dt, db, False) for dt, db in group]
    for copy in seconds:
        copy.start()
    for copy in seconds:
        copy.wait_recv()
    for a_ in range(outer):
        total = sum1[time, b, a_].astype(F32)
        for slot in range(len(group)):
            total = total + got2[slot, a_].astype(F32)
        sum2[a_] = total.astype(BF16)

    base = 1 + len(group)
    thirds = []
    for step in range(1, outer):
        a_ = (a + step) % outer
        thirds.append(remote(sum2.at[a_], got3.at[step - 1], base + step - 1, (time, index_of(a_, b, core))))
    for copy in thirds:
        copy.start()
    for copy in thirds:
        copy.wait_recv()
    total = sum2[a].astype(F32)
    for step in range(1, outer):
        total = total + got3[step - 1].astype(F32)
    part[...] = (total * factor).astype(BF16)
    final[time] = part[...]

    base = base + outer - 1
    lasts = []
    for t in range(1, n_time):
        lasts.append((t, remote(part, final.at[time], base + t - 1, ((time + t) % n_time, height))))
    for _, copy in lasts:
        copy.start()
    for t, _ in lasts:
        sender = (time + n_time - t) % n_time
        remote(part, final.at[sender], base + t - 1, (sender, height)).wait_recv()
    whole = jnp.concatenate([final[t] for t in range(n_time)], axis=1)
    wgrad[...] = whole[:, : wgrad.shape[1]]

    for copy in seconds + thirds + [c for _, c in lasts]:
        copy.wait_send()
    for step in range(1, n_rows):
        sender = (height + n_rows - step) % n_rows
        block(step, sender, sender).wait_recv()
        block(step, height, (height + step) % n_rows).wait_send()


def local(activations, norm_gain, norm_bias, conv_weight, cotangent):
    frames, rows, width, channels = activations.shape
    depth, n_out = conv_weight.shape
    n_time, n_rows = lax.axis_size("tm"), lax.axis_size("height")
    n_dev = n_time * n_rows
    inner = 2
    outer = n_rows // (2 * inner)
    own_rows = n_out // n_rows
    dims = (n_time, n_rows, outer, inner)
    span = -(-depth // (128 * n_time)) * 128
    dma = pltpu.SemaphoreType.DMA

    full, scale = pl.pallas_call(
        functools.partial(gather_kernel, n_time, n_rows),
        out_shape=(
            jax.ShapeDtypeStruct((2 * frames, rows + 2, width, channels), BF16),
            jax.ShapeDtypeStruct((8, channels), F32),
        ),
        in_specs=[VMEM],
        out_specs=(VMEM, VMEM),
        scratch_shapes=[
            pltpu.VMEM((8, channels), F32),
            pltpu.VMEM((n_dev, 8, channels), F32),
            dma((5,)),
            dma((5,)),
            dma((n_dev,)),
            dma((n_dev,)),
        ],
        compiler_params=pltpu.CompilerParams(collective_id=0, has_side_effects=True, vmem_limit_bytes=40 << 20),
        name="gather",
    )(activations)

    pooled, grad = pl.pallas_call(
        functools.partial(compute_kernel, dims),
        out_shape=(
            jax.ShapeDtypeStruct((n_rows, rows, own_rows, width), BF16),
            jax.ShapeDtypeStruct((2, n_time, inner, outer, own_rows, span), BF16),
        ),
        in_specs=[VMEM] * 6,
        out_specs=(VMEM, VMEM),
        scratch_shapes=[
            pltpu.VMEM((KT, (rows + 2) * width, KT * channels), BF16),
            pltpu.VMEM((n_out, rows * width), BF16),
        ],
        compiler_params=pltpu.CompilerParams(vmem_limit_bytes=48 << 20),
        name="compute",
    )(
        full,
        scale,
        norm_gain.reshape(1, channels),
        norm_bias.reshape(1, channels),
        conv_weight,
        cotangent.reshape(rows, width, n_out),
    )

    factor = 0.5 / math.sqrt(frames * n_time * rows * n_rows * width)
    n_sems = n_time * inner + outer + n_time
    out, weight_grad = pl.pallas_call(
        functools.partial(scatter_kernel, dims, factor),
        out_shape=(
            jax.ShapeDtypeStruct((rows * n_rows, own_rows, width), BF16),
            jax.ShapeDtypeStruct((own_rows, depth), BF16),
        ),
        in_specs=[VMEM, VMEM],
        out_specs=(VMEM, VMEM),
        scratch_shapes=[
            pltpu.VMEM((n_time, inner, outer, own_rows, span), BF16),
            pltpu.VMEM((n_time, inner, outer, own_rows, span), BF16),
            pltpu.VMEM((n_time * inner - 1, outer, own_rows, span), BF16),
            pltpu.VMEM((outer, own_rows, span), BF16),
            pltpu.VMEM((outer - 1, own_rows, span), BF16),
            pltpu.VMEM((own_rows, span), BF16),
            dma((n_rows,)),
            dma((n_rows,)),
            dma((n_sems,)),
            dma((n_sems,)),
            pltpu.VMEM((n_time, own_rows, span), BF16),
        ],
        compiler_params=pltpu.CompilerParams(collective_id=1, has_side_effects=True, vmem_limit_bytes=40 << 20),
        name="scatter",
    )(pooled, grad)
    return (out.reshape((1,) + out.shape), weight_grad)


def solution(mesh):
    in_specs = (P("tm", "height", None, None), P(), P(), P(), P("tm", "height", None, None))
    out_specs = (P("tm", None, "height", None), P("height", None))
    return jax.shard_map(local, mesh=mesh, in_specs=in_specs, out_specs=out_specs, check_vma=False)
```

```python
import functools
import math

import jax
import jax.numpy as jnp
from jax import lax
from jax.experimental import pallas as pl
from jax.experimental.pallas import tpu as pltpu
from jax.sharding import PartitionSpec as P

GROUPS = 32
KT = 3
MESH = pl.DeviceIdType.MESH
ANY = pl.BlockSpec(memory_space=pl.ANY)
VMEM = pl.BlockSpec(memory_space=pltpu.VMEM)
BF16 = jnp.bfloat16
F32 = jnp.float32


def group_total(row, per_group):
    lane = lax.broadcasted_iota(jnp.int32, row.shape, 1)
    count = row.shape[1]
    span = 1
    while span < per_group:
        low = (lane % (2 * span)) < span
        row = row + jnp.where(low, pltpu.roll(row, count - span, 1), pltpu.roll(row, span, 1))
        span *= 2
    return row


def index_of(inner, a, b, core):
    return (a * inner + b) * 2 + core


class Stream:
    def __init__(self, dims, place, refs, sems):
        self.dims, self.place = dims, place
        self.grad, self.got1, self.sum1, self.got2, self.sum2, self.got3, self.part, self.final = refs
        self.send_sem, self.recv_sem = sems

    def remote(self, src, dst, index, to):
        return pltpu.make_async_remote_copy(
            src_ref=src,
            dst_ref=dst,
            send_sem=self.send_sem.at[index],
            recv_sem=self.recv_sem.at[index],
            device_id=to,
            device_id_type=MESH,
        )

    def start_pair(self):
        n_time, n_rows, outer, inner = self.dims
        time, height, a, b, core = self.place
        self.pair = self.remote(self.grad.at[1 - core], self.got1, 0, (time, index_of(inner, a, b, 1 - core)))
        self.pair.start()

    def start_second(self):
        n_time, n_rows, outer, inner = self.dims
        time, height, a, b, core = self.place
        self.pair.wait()
        for t in range(n_time):
            for b_ in range(inner):
                for a_ in range(outer):
                    self.sum1[t, b_, a_] = (
                        self.grad[core, t, b_, a_].astype(F32) + self.got1[t, b_, a_].astype(F32)
                    ).astype(BF16)
        self.seconds = []
        for dt in range(n_time):
            for db in range(inner):
                if dt or db:
                    slot = dt * inner + db - 1
                    t_, b_ = (time + dt) % n_time, (b + db) % inner
                    self.seconds.append(
                        self.remote(
                            self.sum1.at[t_, b_], self.got2.at[slot], 1 + slot, (t_, index_of(inner, a, b_, core))
                        )
                    )
        for copy in self.seconds:
            copy.start()

    def start_third(self):
        n_time, n_rows, outer, inner = self.dims
        time, height, a, b, core = self.place
        for copy in self.seconds:
            copy.wait_recv()
        for a_ in range(outer):
            total = self.grad[core, time, b, a_].astype(F32) + self.got1[time, b, a_].astype(F32)
            for slot in range(n_time * inner - 1):
                total = total + self.got2[slot, a_].astype(F32)
            self.sum2[a_] = total.astype(BF16)
        self.thirds = []
        for step in range(1, outer):
            a_ = (a + step) % outer
            self.thirds.append(
                self.remote(
                    self.sum2.at[a_],
                    self.got3.at[step - 1],
                    n_time * inner + step - 1,
                    (time, index_of(inner, a_, b, core)),
                )
            )
        for copy in self.thirds:
            copy.start()

    def start_last(self, factor):
        n_time, n_rows, outer, inner = self.dims
        time, height, a, b, core = self.place
        for copy in self.thirds:
            copy.wait_recv()
        total = self.sum2[a].astype(F32)
        for step in range(1, outer):
            total = total + self.got3[step - 1].astype(F32)
        self.part[...] = (total * factor).astype(BF16)
        self.final[time] = self.part[...]
        self.base = n_time * inner + outer - 1
        self.lasts = []
        for t in range(1, n_time):
            self.lasts.append(
                self.remote(self.part, self.final.at[time], self.base + t - 1, ((time + t) % n_time, height))
            )
        for copy in self.lasts:
            copy.start()

    def finish(self):
        n_time = self.dims[0]
        time, height = self.place[:2]
        for t in range(1, n_time):
            sender = (time + n_time - t) % n_time
            self.remote(self.part, self.final.at[sender], self.base + t - 1, (sender, height)).wait_recv()
        whole = jnp.concatenate([self.final[t] for t in range(n_time)], axis=1)
        for copy in self.seconds + self.thirds + self.lasts:
            copy.wait_send()
        return whole


def block_kernel(dims, factor, act, gain_in, bias_in, weight_in, cot_in, out, wgrad, *scratch):
    n_time, n_rows, outer, inner = dims
    full, first, taps, acc, gain, bias, weight, cot, cot_t, mine, stats, pooled = scratch[:12]
    local_sem, halo_send, halo_recv, stat_send, stat_recv, block_send, block_recv = scratch[12:19]
    late_refs, late_sems = scratch[19:27], scratch[27:29]
    early_refs, early_sems = scratch[29:37], scratch[37:39]
    time, height = lax.axis_index("tm"), lax.axis_index("height")
    frames, rows, width, channels = act.shape
    n_out = weight.shape[1]
    own_rows = n_out // n_rows
    pixels = rows * width
    n_dev = n_time * n_rows
    me = time * n_rows + height
    core, q = height % 2, height // 2
    place = (time, height, q // inner, q % inner, core)
    late = Stream(dims, place, late_refs, late_sems)
    early = Stream(dims, place, early_refs, early_sems)

    own_frames, old_frames = pl.ds(frames, frames), pl.ds(0, frames)
    loads = [
        pltpu.make_async_copy(act, full.at[own_frames, pl.ds(1, rows)], local_sem.at[0]),
        pltpu.make_async_copy(gain_in, gain, local_sem.at[1]),
        pltpu.make_async_copy(bias_in, bias, local_sem.at[2]),
        pltpu.make_async_copy(cot_in, cot, local_sem.at[3]),
        pltpu.make_async_copy(weight_in, weight, local_sem.at[4]),
    ]
    for load in loads:
        load.start()

    barrier = pltpu.get_barrier_semaphore()

    def greet(step, carry):
        other = (me + step) % n_dev
        pl.semaphore_signal(barrier, inc=1, device_id=(other // n_rows, other % n_rows), device_id_type=MESH)
        return carry

    lax.fori_loop(1, n_dev, greet, 0)

    loads[0].wait()
    local = frames * pixels
    chan_sum = jnp.zeros((1, channels), F32)
    for f in range(frames):
        for r in range(rows):
            chan_sum = chan_sum + jnp.sum(full[frames + f, 1 + r].astype(F32), axis=0, keepdims=True)
    chan_mean = chan_sum * (1.0 / local)
    chan_dev = jnp.zeros((1, channels), F32)
    for f in range(frames):
        for r in range(rows):
            away = full[frames + f, 1 + r].astype(F32) - chan_mean
            chan_dev = chan_dev + jnp.sum(away * away, axis=0, keepdims=True)
    packed = jnp.concatenate([chan_mean, chan_dev, jnp.zeros((6, channels), F32)], axis=0)
    mine[...] = packed
    stats[me] = packed
    pl.semaphore_wait(barrier, n_dev - 1)

    def stat(step, slot, to_time, to_height):
        return pltpu.make_async_remote_copy(
            src_ref=mine,
            dst_ref=stats.at[slot],
            send_sem=stat_send.at[step],
            recv_sem=stat_recv.at[step],
            device_id=(to_time, to_height),
            device_id_type=MESH,
        )

    def stat_out(step):
        return stat(step, me, (time + step // n_rows) % n_time, (height + step % n_rows) % n_rows)

    def send(step, carry):
        stat_out(step).start()
        return carry

    has_up, has_down = height > 0, height < n_rows - 1
    has_next, has_prev = time < n_time - 1, time > 0
    moves = [
        (own_frames, 1, 1, old_frames, 1, 1, 0, has_next, has_prev),
        (own_frames, rows, 1, old_frames, rows, 1, 0, has_next, has_prev),
        (own_frames, 2, rows - 2, old_frames, 2, 1, 0, has_next, has_prev),
        (own_frames, 1, 1, own_frames, rows + 1, 0, -1, has_up, has_down),
        (own_frames, rows, 1, own_frames, 0, 0, 1, has_down, has_up),
        (old_frames, 1, 1, old_frames, rows + 1, 0, -1, has_prev & has_up, has_prev & has_down),
        (old_frames, rows, 1, old_frames, 0, 0, 1, has_prev & has_down, has_prev & has_up),
    ]

    def halo(index):
        from_frames, from_row, count, to_frames, to_row, frame_step, row_step = moves[index][:7]
        return pltpu.make_async_remote_copy(
            src_ref=full.at[from_frames, pl.ds(from_row, count)],
            dst_ref=full.at[to_frames, pl.ds(to_row, count)],
            send_sem=halo_send.at[index],
            recv_sem=halo_recv.at[index],
            device_id=(time + frame_step, height + row_step),
            device_id_type=MESH,
        )

    def start(index):
        pl.when(moves[index][7])(lambda: halo(index).start())

    def arrived(index):
        pl.when(moves[index][8])(lambda: halo(index).wait_recv())

    lax.fori_loop(n_rows, n_dev, send, 0)
    for index in range(5):
        start(index)
    lax.fori_loop(1, n_rows, send, 0)

    zero_rows = jnp.zeros((2 * frames, 1, width, channels), BF16)

    @pl.when(jnp.logical_not(has_up))
    def _():
        full[:, pl.ds(0, 1)] = zero_rows

    @pl.when(jnp.logical_not(has_down))
    def _():
        full[:, pl.ds(rows + 1, 1)] = zero_rows

    loads[3].wait()
    for y in range(rows):
        cot_t[:, y * width : (y + 1) * width] = cot[y].astype(F32).T.astype(BF16)
    for index in (1, 2, 4):
        loads[index].wait()

    def receive(step, carry):
        from_time = (time + n_time - step // n_rows) % n_time
        from_height = (height + n_rows - step % n_rows) % n_rows
        stat(step, from_time * n_rows + from_height, from_time, from_height).wait_recv()
        return carry

    lax.fori_loop(1, n_dev, receive, 0)
    per_group = channels // GROUPS
    means, devs = stats[:, 0], stats[:, 1]
    mean = group_total(jnp.sum(means, axis=0, keepdims=True), per_group) * (1.0 / (n_dev * per_group))
    away = means - mean
    spread = jnp.sum(devs + local * (away * away), axis=0, keepdims=True)
    var = group_total(spread, per_group) * (1.0 / (local * n_dev * per_group))
    scale = lax.rsqrt(var + 1e-06) * gain[...]
    shift = bias[...]
    column = lax.broadcasted_iota(jnp.int32, (width, channels), 0)

    def normed(f, r):
        inside = jnp.logical_and(r + height > 0, r + height * rows < n_rows * rows + 1)
        v = (full[f, r].astype(F32) - mean) * scale + shift
        v = v / (1.0 + jnp.exp(-v))
        return v.astype(BF16).astype(F32) * inside.astype(F32)

    def put(t, r, pair):
        left = jnp.where(column == 0, 0.0, pltpu.roll(pair, 1, 0))
        right = jnp.where(column == width - 1, 0.0, pltpu.roll(pair, width - 1, 0))
        base = pl.ds(pl.multiple_of(r * width, width), width)
        taps[t, base, 0:channels] = left.astype(BF16)
        taps[t, base, channels : 2 * channels] = pair.astype(BF16)
        taps[t, base, 2 * channels :] = right.astype(BF16)

    def prepare_own(r, carry):
        one, two = normed(frames, r), normed(frames + 1, r)
        first[r] = one.astype(BF16)
        put(2, r, one + two)
        return carry

    arrived(3)
    arrived(4)
    lax.fori_loop(0, rows + 2, prepare_own, 0)

    def product(stream, t, offset, length):
        band = KT * KT * channels
        span = stream.grad.shape[-1]
        rhs = jnp.concatenate([taps[t, pl.ds(r * width, pixels)] for r in range(KT)], axis=1)
        total = jnp.dot(cot_t[...], rhs, preferred_element_type=F32).astype(BF16)
        for piece in range(n_time):
            begin, end = max(offset, piece * span), min(offset + band, (piece + 1) * span)
            if begin < end:
                part = total[:, begin - offset : end - offset]
                for block in range(n_rows):
                    q_, core_ = block // 2, block % 2
                    stream.grad[
                        core_, piece, q_ % inner, q_ // inner, :, begin - piece * span : end - piece * span
                    ] = part[block * own_rows : (block + 1) * own_rows]
            unused = max(length, piece * span) - piece * span
            if offset + band == length and unused < span:
                stream.grad[:, piece, :, :, :, unused:] = jnp.zeros((2, inner, outer, own_rows, span - unused), BF16)

    band = KT * KT * channels
    product(early, 2, 0, band)
    early.start_pair()

    arrived(0)
    start(5)
    arrived(1)
    start(6)

    def patch(t, y):
        return [taps[t, pl.ds(pl.multiple_of((y + r) * width, width), width)] for r in range(KT)]

    def conv_own(y, carry):
        acc[y] = jnp.dot(jnp.concatenate(patch(2, y), axis=1), weight[2 * band :], preferred_element_type=F32)
        return carry

    lax.fori_loop(0, rows, conv_own, 0)
    early.start_second()

    for index in (2, 5, 6):
        arrived(index)

    @pl.when(jnp.logical_not(has_prev))
    def _():
        for f in range(frames):
            full[f] = full[frames]

    def prepare_old(r, carry):
        one, two = normed(0, r), normed(1, r)
        put(0, r, one + two)
        put(1, r, two + first[r].astype(F32))
        return carry

    lax.fori_loop(0, rows + 2, prepare_old, 0)

    def conv_old(y, carry):
        lhs = jnp.concatenate(patch(0, y) + patch(1, y), axis=1)
        total = (acc[y] + jnp.dot(lhs, weight[0 : 2 * band], preferred_element_type=F32)) * 0.5
        pooled[:, y] = total.T.astype(BF16).reshape(n_rows, own_rows, width)
        return carry

    lax.fori_loop(0, rows, conv_old, 0)

    def block(step, slot, other):
        return pltpu.make_async_remote_copy(
            src_ref=pooled.at[other],
            dst_ref=out.at[pl.ds(slot * rows, rows)],
            send_sem=block_send.at[step],
            recv_sem=block_recv.at[step],
            device_id=(time, other),
            device_id_type=MESH,
        )

    for step in range(1, n_rows):
        block(step, height, (height + step) % n_rows).start()
    product(late, 0, 0, 2 * band)
    product(late, 1, band, 2 * band)
    late.start_pair()
    out[pl.ds(height * rows, rows)] = pooled[height]
    early.start_third()
    late.start_second()
    early.start_last(factor)
    late.start_third()
    wgrad[:, 2 * band :] = early.finish()[:, :band]
    late.start_last(factor)
    wgrad[:, : 2 * band] = late.finish()[:, : 2 * band]

    for step in range(1, n_rows):
        sender = (height + n_rows - step) % n_rows
        block(step, sender, sender).wait_recv()
        block(step, height, (height + step) % n_rows).wait_send()
    for index in range(len(moves)):
        pl.when(moves[index][7])(functools.partial(lambda i: halo(i).wait_send(), index))

    def sent(step, carry):
        stat_out(step).wait_send()
        return carry

    lax.fori_loop(1, n_dev, sent, 0)


def local(activations, norm_gain, norm_bias, conv_weight, cotangent):
    frames, rows, width, channels = activations.shape
    depth, n_out = conv_weight.shape
    n_time, n_rows = lax.axis_size("tm"), lax.axis_size("height")
    n_dev = n_time * n_rows
    inner = 2
    outer = n_rows // (2 * inner)
    own_rows = n_out // n_rows
    dims = (n_time, n_rows, outer, inner)
    dma = pltpu.SemaphoreType.DMA
    factor = 0.5 / math.sqrt(frames * n_time * rows * n_rows * width)

    def stream(length):
        span = -(-length // (128 * n_time)) * 128
        n_sems = n_time * inner + outer + n_time
        shapes = [
            (2, n_time, inner, outer, own_rows, span),
            (n_time, inner, outer, own_rows, span),
            (n_time, inner, outer, own_rows, span),
            (n_time * inner - 1, outer, own_rows, span),
            (outer, own_rows, span),
            (outer - 1, own_rows, span),
            (own_rows, span),
            (n_time, own_rows, span),
        ]
        return [pltpu.VMEM(shape, BF16) for shape in shapes] + [dma((n_sems,)), dma((n_sems,))]

    band = depth // KT
    out, weight_grad = pl.pallas_call(
        functools.partial(block_kernel, dims, factor),
        out_shape=(
            jax.ShapeDtypeStruct((rows * n_rows, own_rows, width), BF16),
            jax.ShapeDtypeStruct((own_rows, depth), BF16),
        ),
        in_specs=[ANY] * 5,
        out_specs=(VMEM, VMEM),
        scratch_shapes=[
            pltpu.VMEM((2 * frames, rows + 2, width, channels), BF16),
            pltpu.VMEM((rows + 2, width, channels), BF16),
            pltpu.VMEM((KT, (rows + 2) * width, KT * channels), BF16),
            pltpu.VMEM((rows, width, n_out), F32),
            pltpu.VMEM((1, channels), F32),
            pltpu.VMEM((1, channels), F32),
            pltpu.VMEM((depth, n_out), BF16),
            pltpu.VMEM((rows, width, n_out), BF16),
            pltpu.VMEM((n_out, rows * width), BF16),
            pltpu.VMEM((8, channels), F32),
            pltpu.VMEM((n_dev, 8, channels), F32),
            pltpu.VMEM((n_rows, rows, own_rows, width), BF16),
            dma((5,)),
            dma((7,)),
            dma((7,)),
            dma((n_dev,)),
            dma((n_dev,)),
            dma((n_rows,)),
            dma((n_rows,)),
            *stream(2 * band),
            *stream(band),
        ],
        compiler_params=pltpu.CompilerParams(collective_id=0, has_side_effects=True, vmem_limit_bytes=56 << 20),
        name="block",
    )(
        activations,
        norm_gain.reshape(1, channels),
        norm_bias.reshape(1, channels),
        conv_weight,
        cotangent.reshape(rows, width, n_out),
    )
    return (out.reshape((1,) + out.shape), weight_grad)


def solution(mesh):
    in_specs = (P("tm", "height", None, None), P(), P(), P(), P("tm", "height", None, None))
    out_specs = (P("tm", None, "height", None), P("height", None))
    return jax.shard_map(local, mesh=mesh, in_specs=in_specs, out_specs=out_specs, check_vma=False)
```

```python
import functools
import math

import jax
import jax.numpy as jnp
from jax import lax
from jax.experimental import pallas as pl
from jax.experimental.pallas import tpu as pltpu
from jax.sharding import PartitionSpec as P

GROUPS = 32
KT = 3
CUTS = 2
MESH = pl.DeviceIdType.MESH
ANY = pl.BlockSpec(memory_space=pl.ANY)
VMEM = pl.BlockSpec(memory_space=pltpu.VMEM)
BF16 = jnp.bfloat16
F32 = jnp.float32


def group_total(row, per_group):
    lane = lax.broadcasted_iota(jnp.int32, row.shape, 1)
    count = row.shape[1]
    span = 1
    while span < per_group:
        low = (lane % (2 * span)) < span
        row = row + jnp.where(low, pltpu.roll(row, count - span, 1), pltpu.roll(row, span, 1))
        span *= 2
    return row


def index_of(inner, a, b, core):
    return (a * inner + b) * 2 + core


class Stream:
    def __init__(self, dims, place, refs, sems):
        self.dims, self.place = dims, place
        self.grad, self.got1, self.sum1, self.got2, self.sum2, self.got3, self.part, self.final = refs
        self.send_sem, self.recv_sem = sems

    def remote(self, src, dst, index, to):
        return pltpu.make_async_remote_copy(
            src_ref=src,
            dst_ref=dst,
            send_sem=self.send_sem.at[index],
            recv_sem=self.recv_sem.at[index],
            device_id=to,
            device_id_type=MESH,
        )

    def start_pair(self):
        n_time, n_rows, outer, inner = self.dims
        time, height, a, b, core = self.place
        self.pair = self.remote(self.grad.at[1 - core], self.got1, 0, (time, index_of(inner, a, b, 1 - core)))
        self.pair.start()

    def start_second(self):
        n_time, n_rows, outer, inner = self.dims
        time, height, a, b, core = self.place
        self.pair.wait()
        for t in range(n_time):
            for b_ in range(inner):
                for a_ in range(outer):
                    self.sum1[t, b_, a_] = (
                        self.grad[core, t, b_, a_].astype(F32) + self.got1[t, b_, a_].astype(F32)
                    ).astype(BF16)
        self.seconds = []
        for dt in range(n_time):
            for db in range(inner):
                if dt or db:
                    slot = dt * inner + db - 1
                    t_, b_ = (time + dt) % n_time, (b + db) % inner
                    self.seconds.append(
                        self.remote(
                            self.sum1.at[t_, b_], self.got2.at[slot], 1 + slot, (t_, index_of(inner, a, b_, core))
                        )
                    )
        for copy in self.seconds:
            copy.start()

    def start_third(self):
        n_time, n_rows, outer, inner = self.dims
        time, height, a, b, core = self.place
        for copy in self.seconds:
            copy.wait_recv()
        for a_ in range(outer):
            total = self.grad[core, time, b, a_].astype(F32) + self.got1[time, b, a_].astype(F32)
            for slot in range(n_time * inner - 1):
                total = total + self.got2[slot, a_].astype(F32)
            self.sum2[a_] = total.astype(BF16)
        self.thirds = []
        for step in range(1, outer):
            a_ = (a + step) % outer
            self.thirds.append(
                self.remote(
                    self.sum2.at[a_],
                    self.got3.at[step - 1],
                    n_time * inner + step - 1,
                    (time, index_of(inner, a_, b, core)),
                )
            )
        for copy in self.thirds:
            copy.start()

    def start_last(self, factor):
        n_time, n_rows, outer, inner = self.dims
        time, height, a, b, core = self.place
        for copy in self.thirds:
            copy.wait_recv()
        total = self.sum2[a].astype(F32)
        for step in range(1, outer):
            total = total + self.got3[step - 1].astype(F32)
        self.part[...] = (total * factor).astype(BF16)
        self.final[time] = self.part[...]
        self.base = n_time * inner + outer - 1
        self.lasts = []
        for t in range(1, n_time):
            self.lasts.append(
                self.remote(self.part, self.final.at[time], self.base + t - 1, ((time + t) % n_time, height))
            )
        for copy in self.lasts:
            copy.start()

    def finish(self):
        n_time = self.dims[0]
        time, height = self.place[:2]
        for t in range(1, n_time):
            sender = (time + n_time - t) % n_time
            self.remote(self.part, self.final.at[sender], self.base + t - 1, (sender, height)).wait_recv()
        whole = jnp.concatenate([self.final[t] for t in range(n_time)], axis=1)
        for copy in self.seconds + self.thirds + self.lasts:
            copy.wait_send()
        return whole


def block_kernel(dims, factor, act, gain_in, bias_in, weight_in, cot_in, out, wgrad, *scratch):
    n_time, n_rows, outer, inner = dims
    full, first, taps, acc, gain, bias, weight, cot, cot_t, mine, stats, pooled = scratch[:12]
    local_sem, halo_send, halo_recv, stat_send, stat_recv, block_send, block_recv = scratch[12:19]
    late_refs, late_sems = scratch[19:27], scratch[27:29]
    early_refs, early_sems = scratch[29:37], scratch[37:39]
    time, height = lax.axis_index("tm"), lax.axis_index("height")
    frames, rows, width, channels = act.shape
    n_out = weight.shape[1]
    own_rows = n_out // n_rows
    pixels = rows * width
    n_dev = n_time * n_rows
    me = time * n_rows + height
    core, q = height % 2, height // 2
    place = (time, height, q // inner, q % inner, core)
    late = Stream(dims, place, late_refs, late_sems)
    early = Stream(dims, place, early_refs, early_sems)

    own_frames, old_frames = pl.ds(frames, frames), pl.ds(0, frames)
    loads = [
        pltpu.make_async_copy(act, full.at[own_frames, pl.ds(1, rows)], local_sem.at[0]),
        pltpu.make_async_copy(gain_in, gain, local_sem.at[1]),
        pltpu.make_async_copy(bias_in, bias, local_sem.at[2]),
        pltpu.make_async_copy(cot_in, cot, local_sem.at[3]),
        pltpu.make_async_copy(weight_in, weight, local_sem.at[4]),
    ]
    for load in loads:
        load.start()

    barrier = pltpu.get_barrier_semaphore()

    def greet(step, carry):
        other = (me + step) % n_dev
        pl.semaphore_signal(barrier, inc=1, device_id=(other // n_rows, other % n_rows), device_id_type=MESH)
        return carry

    lax.fori_loop(1, n_dev, greet, 0)

    loads[0].wait()
    local = frames * pixels
    chan_sum = jnp.zeros((1, channels), F32)
    for f in range(frames):
        for r in range(rows):
            chan_sum = chan_sum + jnp.sum(full[frames + f, 1 + r].astype(F32), axis=0, keepdims=True)
    chan_mean = chan_sum * (1.0 / local)
    chan_dev = jnp.zeros((1, channels), F32)
    for f in range(frames):
        for r in range(rows):
            away = full[frames + f, 1 + r].astype(F32) - chan_mean
            chan_dev = chan_dev + jnp.sum(away * away, axis=0, keepdims=True)
    packed = jnp.concatenate([chan_mean, chan_dev, jnp.zeros((6, channels), F32)], axis=0)
    mine[...] = packed
    stats[me] = packed
    pl.semaphore_wait(barrier, n_dev - 1)

    def stat(step, slot, to_time, to_height):
        return pltpu.make_async_remote_copy(
            src_ref=mine,
            dst_ref=stats.at[slot],
            send_sem=stat_send.at[step],
            recv_sem=stat_recv.at[step],
            device_id=(to_time, to_height),
            device_id_type=MESH,
        )

    def stat_out(step):
        return stat(step, me, (time + step // n_rows) % n_time, (height + step % n_rows) % n_rows)

    def send(step, carry):
        stat_out(step).start()
        return carry

    has_up, has_down = height > 0, height < n_rows - 1
    has_next, has_prev = time < n_time - 1, time > 0
    moves = [
        (own_frames, 1, 1, old_frames, 1, 1, 0, has_next, has_prev),
        (own_frames, rows, 1, old_frames, rows, 1, 0, has_next, has_prev),
        (own_frames, 2, rows - 2, old_frames, 2, 1, 0, has_next, has_prev),
        (own_frames, 1, 1, own_frames, rows + 1, 0, -1, has_up, has_down),
        (own_frames, rows, 1, own_frames, 0, 0, 1, has_down, has_up),
        (old_frames, 1, 1, old_frames, rows + 1, 0, -1, has_prev & has_up, has_prev & has_down),
        (old_frames, rows, 1, old_frames, 0, 0, 1, has_prev & has_down, has_prev & has_up),
    ]

    def halo(index):
        from_frames, from_row, count, to_frames, to_row, frame_step, row_step = moves[index][:7]
        return pltpu.make_async_remote_copy(
            src_ref=full.at[from_frames, pl.ds(from_row, count)],
            dst_ref=full.at[to_frames, pl.ds(to_row, count)],
            send_sem=halo_send.at[index],
            recv_sem=halo_recv.at[index],
            device_id=(time + frame_step, height + row_step),
            device_id_type=MESH,
        )

    def start(index):
        pl.when(moves[index][7])(lambda: halo(index).start())

    def arrived(index):
        pl.when(moves[index][8])(lambda: halo(index).wait_recv())

    lax.fori_loop(n_rows, n_dev, send, 0)
    for index in range(5):
        start(index)
    lax.fori_loop(1, n_rows, send, 0)

    zero_rows = jnp.zeros((2 * frames, 1, width, channels), BF16)

    @pl.when(jnp.logical_not(has_up))
    def _():
        full[:, pl.ds(0, 1)] = zero_rows

    @pl.when(jnp.logical_not(has_down))
    def _():
        full[:, pl.ds(rows + 1, 1)] = zero_rows

    loads[3].wait()
    for y in range(rows):
        cot_t[:, y * width : (y + 1) * width] = cot[y].astype(F32).T.astype(BF16)
    for index in (1, 2, 4):
        loads[index].wait()

    def receive(step, carry):
        from_time = (time + n_time - step // n_rows) % n_time
        from_height = (height + n_rows - step % n_rows) % n_rows
        stat(step, from_time * n_rows + from_height, from_time, from_height).wait_recv()
        return carry

    lax.fori_loop(1, n_dev, receive, 0)
    per_group = channels // GROUPS
    means, devs = stats[:, 0], stats[:, 1]
    mean = group_total(jnp.sum(means, axis=0, keepdims=True), per_group) * (1.0 / (n_dev * per_group))
    away = means - mean
    spread = jnp.sum(devs + local * (away * away), axis=0, keepdims=True)
    var = group_total(spread, per_group) * (1.0 / (local * n_dev * per_group))
    scale = lax.rsqrt(var + 1e-06) * gain[...]
    shift = bias[...]
    column = lax.broadcasted_iota(jnp.int32, (width, channels), 0)

    def normed(f, r):
        inside = jnp.logical_and(r + height > 0, r + height * rows < n_rows * rows + 1)
        v = (full[f, r].astype(F32) - mean) * scale + shift
        v = v / (1.0 + jnp.exp(-v))
        return v.astype(BF16).astype(F32) * inside.astype(F32)

    def put(t, r, pair):
        left = jnp.where(column == 0, 0.0, pltpu.roll(pair, 1, 0))
        right = jnp.where(column == width - 1, 0.0, pltpu.roll(pair, width - 1, 0))
        base = pl.ds(pl.multiple_of(r * width, width), width)
        taps[t, base, 0:channels] = left.astype(BF16)
        taps[t, base, channels : 2 * channels] = pair.astype(BF16)
        taps[t, base, 2 * channels :] = right.astype(BF16)

    def prepare_own(r, carry):
        one, two = normed(frames, r), normed(frames + 1, r)
        first[r] = one.astype(BF16)
        put(2, r, one + two)
        return carry

    arrived(3)
    arrived(4)
    lax.fori_loop(0, rows + 2, prepare_own, 0)

    def product(stream, t, offset, length):
        band = KT * KT * channels
        span = stream.grad.shape[-1]
        rhs = jnp.concatenate([taps[t, pl.ds(r * width, pixels)] for r in range(KT)], axis=1)
        total = jnp.dot(cot_t[...], rhs, preferred_element_type=F32).astype(BF16)
        for piece in range(n_time):
            begin, end = max(offset, piece * span), min(offset + band, (piece + 1) * span)
            if begin < end:
                part = total[:, begin - offset : end - offset]
                for block in range(n_rows):
                    q_, core_ = block // 2, block % 2
                    stream.grad[
                        core_, piece, q_ % inner, q_ // inner, :, begin - piece * span : end - piece * span
                    ] = part[block * own_rows : (block + 1) * own_rows]
            unused = max(length, piece * span) - piece * span
            if offset + band == length and unused < span:
                stream.grad[:, piece, :, :, :, unused:] = jnp.zeros((2, inner, outer, own_rows, span - unused), BF16)

    band = KT * KT * channels
    product(early, 2, 0, band)
    early.start_pair()

    arrived(0)
    start(5)
    arrived(1)
    start(6)

    many = 2 if rows % 2 == 0 else 1

    def patch(t, y):
        return [taps[t, pl.ds(pl.multiple_of((y * many + r) * width, width), many * width)] for r in range(KT)]

    def conv_own(y, carry):
        acc[y] = jnp.dot(jnp.concatenate(patch(2, y), axis=1), weight[2 * band :], preferred_element_type=F32)
        return carry

    lax.fori_loop(0, rows // many, conv_own, 0)
    for index in (2, 5, 6):
        arrived(index)

    @pl.when(jnp.logical_not(has_prev))
    def _():
        for f in range(frames):
            full[f] = full[frames]

    def prepare_old(r, carry):
        one, two = normed(0, r), normed(1, r)
        put(0, r, one + two)
        put(1, r, two + first[r].astype(F32))
        return carry

    lax.fori_loop(0, rows + 2, prepare_old, 0)
    early.start_second()

    def conv_old(y, carry):
        lhs = jnp.concatenate(patch(0, y) + patch(1, y), axis=1)
        total = (acc[y] + jnp.dot(lhs, weight[0 : 2 * band], preferred_element_type=F32)) * 0.5
        for k in range(many):
            part = total[k * width : (k + 1) * width].T.astype(BF16)
            pooled[:, y * many + k] = part.reshape(n_rows, own_rows, width)
        return carry

    lax.fori_loop(0, rows // many, conv_old, 0)

    def block(step, slot, other):
        return pltpu.make_async_remote_copy(
            src_ref=pooled.at[other],
            dst_ref=out.at[pl.ds(slot * rows, rows)],
            send_sem=block_send.at[step],
            recv_sem=block_recv.at[step],
            device_id=(time, other),
            device_id_type=MESH,
        )

    for step in range(1, n_rows):
        block(step, height, (height + step) % n_rows).start()
    product(late, 0, 0, 2 * band)
    product(late, 1, band, 2 * band)
    late.start_pair()
    out[pl.ds(height * rows, rows)] = pooled[height]
    early.start_third()
    late.start_second()
    late.start_third()
    early.start_last(factor)
    wgrad[:, 2 * band :] = early.finish()[:, :band]
    late.start_last(factor)
    wgrad[:, : 2 * band] = late.finish()[:, : 2 * band]

    for step in range(1, n_rows):
        sender = (height + n_rows - step) % n_rows
        block(step, sender, sender).wait_recv()
        block(step, height, (height + step) % n_rows).wait_send()
    for index in range(len(moves)):
        pl.when(moves[index][7])(functools.partial(lambda i: halo(i).wait_send(), index))

    def sent(step, carry):
        stat_out(step).wait_send()
        return carry

    lax.fori_loop(1, n_dev, sent, 0)


def deliver_kernel(block_in, grad_in, block_out, grad_out, block_mid, grad_mid, in_sem, out_sem):
    size = block_in.shape[0] // CUTS
    pieces = [tuple(r.at[pl.ds(i * size, size)] for r in (block_in, block_mid, block_out)) for i in range(CUTS)]
    pieces.append((grad_in, grad_mid, grad_out))
    arrivals, departures = [], []
    for i, (source, middle, target) in enumerate(pieces):
        arrivals.append(pltpu.make_async_copy(source, middle, in_sem.at[i]))
        departures.append(pltpu.make_async_copy(middle, target, out_sem.at[i]))
        arrivals[-1].start()
    for arrival, departure in zip(arrivals, departures):
        arrival.wait()
        departure.start()
    for departure in departures:
        departure.wait()


def local(activations, norm_gain, norm_bias, conv_weight, cotangent):
    frames, rows, width, channels = activations.shape
    depth, n_out = conv_weight.shape
    n_time, n_rows = lax.axis_size("tm"), lax.axis_size("height")
    n_dev = n_time * n_rows
    inner = 2
    outer = n_rows // (2 * inner)
    own_rows = n_out // n_rows
    dims = (n_time, n_rows, outer, inner)
    dma = pltpu.SemaphoreType.DMA
    factor = 0.5 / math.sqrt(frames * n_time * rows * n_rows * width)

    many = 2 if rows % 2 == 0 else 1

    def stream(length):
        span = -(-length // (128 * n_time)) * 128
        n_sems = n_time * inner + outer + n_time
        shapes = [
            (2, n_time, inner, outer, own_rows, span),
            (n_time, inner, outer, own_rows, span),
            (n_time, inner, outer, own_rows, span),
            (n_time * inner - 1, outer, own_rows, span),
            (outer, own_rows, span),
            (outer - 1, own_rows, span),
            (own_rows, span),
            (n_time, own_rows, span),
        ]
        return [pltpu.VMEM(shape, BF16) for shape in shapes] + [dma((n_sems,)), dma((n_sems,))]

    band = depth // KT
    out, weight_grad = pl.pallas_call(
        functools.partial(block_kernel, dims, factor),
        out_shape=(
            jax.ShapeDtypeStruct((rows * n_rows, own_rows, width), BF16),
            jax.ShapeDtypeStruct((own_rows, depth), BF16),
        ),
        in_specs=[ANY] * 5,
        out_specs=(VMEM, VMEM),
        scratch_shapes=[
            pltpu.VMEM((2 * frames, rows + 2, width, channels), BF16),
            pltpu.VMEM((rows + 2, width, channels), BF16),
            pltpu.VMEM((KT, (rows + 2) * width, KT * channels), BF16),
            pltpu.VMEM((rows // many, many * width, n_out), F32),
            pltpu.VMEM((1, channels), F32),
            pltpu.VMEM((1, channels), F32),
            pltpu.VMEM((depth, n_out), BF16),
            pltpu.VMEM((rows, width, n_out), BF16),
            pltpu.VMEM((n_out, rows * width), BF16),
            pltpu.VMEM((8, channels), F32),
            pltpu.VMEM((n_dev, 8, channels), F32),
            pltpu.VMEM((n_rows, rows, own_rows, width), BF16),
            dma((5,)),
            dma((7,)),
            dma((7,)),
            dma((n_dev,)),
            dma((n_dev,)),
            dma((n_rows,)),
            dma((n_rows,)),
            *stream(2 * band),
            *stream(band),
        ],
        compiler_params=pltpu.CompilerParams(collective_id=0, has_side_effects=True, vmem_limit_bytes=56 << 20),
        name="block",
    )(
        activations,
        norm_gain.reshape(1, channels),
        norm_bias.reshape(1, channels),
        conv_weight,
        cotangent.reshape(rows, width, n_out),
    )
    out, weight_grad = pl.pallas_call(
        deliver_kernel,
        out_shape=(
            jax.ShapeDtypeStruct(out.shape, BF16),
            jax.ShapeDtypeStruct(weight_grad.shape, BF16),
        ),
        in_specs=[ANY] * 2,
        out_specs=(ANY, ANY),
        scratch_shapes=[
            pltpu.VMEM(out.shape, BF16),
            pltpu.VMEM(weight_grad.shape, BF16),
            dma((CUTS + 1,)),
            dma((CUTS + 1,)),
        ],
        compiler_params=pltpu.CompilerParams(vmem_limit_bytes=56 << 20),
        name="deliver",
    )(out, weight_grad)
    return (out.reshape((1,) + out.shape), weight_grad)


def solution(mesh):
    in_specs = (P("tm", "height", None, None), P(), P(), P(), P("tm", "height", None, None))
    out_specs = (P("tm", None, "height", None), P("height", None))
    return jax.shard_map(local, mesh=mesh, in_specs=in_specs, out_specs=out_specs, check_vma=False)
```
